32 devices in a mesh: dp: 8 (over z, x), expert: 4 (over y, core).
Axes of the slice: x: 2, y: 2, z: 4, core: 2. Of those that a mesh axis runs over, the one named last changes fastest.
Arguments:
- x_spans: bfloat16 [8, 8, 4, 16, 1536], P('dp', None, 'expert'), may hold values from -36 to 36
- crops: int32 [8, 4, 128, 1], P('dp', 'expert'), may hold values from 0 to 7; in each aligned block of 128 rows (0 to 127, 128 to 255, ..., all dimensions but the last counted through in order) at most 32 rows name the same one
- decay: float32 [8, 4, 128, 24], P('dp', 'expert'), may hold values from -1 to 0
- attn_gain: bfloat16 [1536], replicated, may hold values from 0.099609375 to 1.8984375
- w_query: bfloat16 [1536, 1536], replicated, may hold values from -0.15625 to 0.15625
- w_key: bfloat16 [1536, 1536], replicated, may hold values from -0.15625 to 0.15625
- w_value: bfloat16 [1536, 1536], replicated, may hold values from -0.15625 to 0.15625
- head_gain: bfloat16 [1536], replicated, may hold values from 0.099609375 to 1.8984375
- w_out: bfloat16 [1536, 1536], replicated, may hold values from -0.15625 to 0.15625
- moe_gain: bfloat16 [1536], replicated, may hold values from 0.099609375 to 1.8984375
- w_gate: bfloat16 [8, 1536, 6144], P('expert', None, 'dp'), may hold values from -0.15625 to 0.15625
- w_up: bfloat16 [8, 1536, 6144], P('expert', None, 'dp'), may hold values from -0.15625 to 0.15625
- w_down: bfloat16 [8, 6144, 1536], P('expert', 'dp'), may hold values from -0.078125 to 0.078125
Outputs:
- layer_out: bfloat16 [8, 4, 128, 1536], P('dp', 'expert')
The draws below stay inside these ranges and needn't reach their ends.
Inputs may be any that keep to these rules, and one draw needn't show every extreme that they name: `crops`: within the tokens of one plot no crop is named more than 32 times, and some plot names some crop exactly 32 times.
All inputs are finite; a program needn't handle non-finite values.
Results may differ from the reference program's by a relative error of at most 0.012.
Values may be sent and summed in bfloat16 or wider, within the bound.
A program may use at most 128 MiB of HBM per device.

```python
import math
import jax
import jax.numpy as jnp
import numpy as np
from jax import lax

D = 1536
HEADS = 24
HEAD_DIM = 64
FF = 6144
EXPERTS = 8
VISITS_EACH_TILE = 128
CAP = 32
SPANS = 8
PARCEL_DOWNWARD = 8
PARCEL_ACROSS = 4
PLOTS = 32
CLEN = 16
HID_DEV = 768
N_DP = 8


def draw_x_spans(key, part):
    noise_seed_splits = jax.random.split(key, 3)
    full_shape = (SPANS, PARCEL_DOWNWARD, PARCEL_ACROSS, CLEN, D)
    row_scale = jnp.exp(jax.random.uniform(noise_seed_splits[1], (SPANS, PARCEL_DOWNWARD, PARCEL_ACROSS, CLEN, 1), minval=math.log(0.3), maxval=math.log(3.0)))
    col_scale = jnp.exp(jax.random.uniform(noise_seed_splits[2], (D,), minval=math.log(0.3), maxval=math.log(3.0)))
    noise_base = jax.random.truncated_normal(noise_seed_splits[0], -4.0, 4.0, full_shape)
    return (noise_base * row_scale * col_scale).astype(jnp.bfloat16)


def draw_decay(key, part):
    noise_seed_splits = jax.random.split(key, 7)
    full_shape = (PARCEL_DOWNWARD, PARCEL_ACROSS, VISITS_EACH_TILE, HEADS)
    fast_share = 0.5
    fast_heads = jax.random.uniform(noise_seed_splits[0], (HEADS,)) < fast_share
    fast_rate = jax.random.uniform(noise_seed_splits[1], (HEADS,), minval=1.0 / 50.0, maxval=1.0 / 30.0)
    slow_rate = jax.random.uniform(noise_seed_splits[2], (HEADS,), minval=0.1, maxval=0.4) / VISITS_EACH_TILE
    channel_fading_speed = jnp.where(fast_heads, fast_rate, slow_rate)
    parcel_scaling = jnp.exp(jax.random.uniform(noise_seed_splits[3], (PARCEL_DOWNWARD, PARCEL_ACROSS, 1, HEADS), minval=math.log(0.5), maxval=math.log(2.0)))
    noise_jitter = jax.random.uniform(noise_seed_splits[4], full_shape, minval=0.5, maxval=1.5)
    spike_switched_on = jax.random.uniform(noise_seed_splits[5], (PARCEL_DOWNWARD, PARCEL_ACROSS, VISITS_EACH_TILE, 1)) < 2.0 / VISITS_EACH_TILE
    spike_duration = jax.random.uniform(noise_seed_splits[6], (PARCEL_DOWNWARD, PARCEL_ACROSS, VISITS_EACH_TILE, 1), minval=0.22, maxval=0.69)
    return (-(channel_fading_speed * parcel_scaling * noise_jitter) - jnp.where(spike_switched_on, spike_duration, 0.0)).astype(jnp.float32)


def block_levels(rng, shape, shards, least, largest):
    def one(dim, blocks):
        draws = jax.random.uniform(jax.random.fold_in(jax.random.fold_in(rng, 6), dim), (blocks,), jnp.float32, least / len(shards), largest / len(shards))
        return jnp.repeat(jnp.exp(draws), shape[dim] // blocks).reshape((-1,) + (1,) * (len(shape) - dim - 1))

    level = one(*shards[0])
    for cut in shards[1:]:
        level = level * one(*cut)
    return level


def routed_block(stream_key, own, number, rows, amount, top, reach, skew):
    sequence = jax.random.permutation(stream_key, amount)
    heavy_load, usual = load_shares(amount, rows * top, reach, skew, True), load_shares(amount, rows * top, reach, skew, False)
    places = jnp.arange(amount)

    def named(tallies, turn):
        used = int((tallies > 0).sum())
        fixed = max(1, used // 4)
        shifted = fixed + (places - fixed + turn * (used - fixed)) % max(1, amount - fixed)
        return jnp.zeros((amount,), jnp.int32).at[sequence[jnp.where(places < fixed, places, shifted)]].set(jnp.asarray(tallies, jnp.int32))

    tallies = jnp.where(number % 4 == 0, named(heavy_load, number // 4), named(usual, number - number // 4 - 1))
    mixed = jax.random.permutation(jax.random.fold_in(own, 3), amount)
    donor, receiver = mixed[0:amount // 2 * 2:2], mixed[1:amount // 2 * 2:2]
    margin = jnp.minimum(tallies[donor] - 1, reach - tallies[receiver]) // 2
    margin = jnp.where((donor == sequence[0]) | (receiver == sequence[0]) | (tallies[receiver] == 0), 0, jnp.maximum(margin, 0))
    shifted = jax.random.randint(jax.random.fold_in(own, 4), (amount // 2,), 0, 1 << 20) % (margin + 1)
    tallies = tallies.at[donor].add(-shifted).at[receiver].add(shifted)
    members = jnp.searchsorted(jnp.cumsum(tallies), jnp.arange(rows * top), side="right").astype(jnp.int32)
    table = members.reshape(top, rows).T
    table = table[jax.random.permutation(jax.random.fold_in(own, 1), rows)]
    turn = jax.random.randint(jax.random.fold_in(own, 2), (rows, 1), 0, top)
    return jnp.take_along_axis(table, (jnp.arange(top)[None, :] + turn) % top, axis=1)


def load_shares(count, total, bound, slope, full):
    portions = [(1 << 20) // math.isqrt(rank ** slope) + 1 for rank in range(1, count + 1)]
    largest = bound if full else min(bound, max(-(-total // count), total * portions[0] // sum(portions)))
    least = 1 if total - largest >= count - 1 else 0
    counts, rest = [largest] + [least] * (count - 1), total - largest - least * (count - 1)
    while rest > 0:
        free = [i for i in range(1, count) if counts[i] < largest] or [i for i in range(1, count) if counts[i] < bound]
        whole, left = sum([portions[i] for i in free]), rest
        for i in free:
            addition = min(bound - counts[i], max(1, left * portions[i] // whole), rest)
            counts[i] = counts[i] + addition
            rest = rest - addition
    return np.array(counts)


def normal_values(key, shape, spread, reach, cuts=(), kind=jnp.bfloat16):
    result = jax.random.normal(key, shape, jnp.float32) * spread
    if len(cuts) > 0:
        result = block_levels(key, shape, cuts, -0.22, 0.18) * result
    return jnp.clip(result, min=-reach, max=reach).astype(kind)


def setup_inputs(seed: int = 0) -> dict:
    arg_keys = jax.random.split(jax.random.key(seed), 14)
    x_spans = draw_x_spans(jax.random.fold_in(arg_keys[13], 71), 0)
    crops_keys = jax.random.split(jax.random.fold_in(arg_keys[1], 1), PARCEL_DOWNWARD * PARCEL_ACROSS * VISITS_EACH_TILE // VISITS_EACH_TILE)
    crops_turns = jax.random.permutation(jax.random.fold_in(arg_keys[1], 3), PARCEL_DOWNWARD * PARCEL_ACROSS * VISITS_EACH_TILE // VISITS_EACH_TILE)
    crops = jax.vmap(lambda own, number: routed_block(jax.random.fold_in(arg_keys[1], 2), own, number, VISITS_EACH_TILE, EXPERTS, 1, CAP, 2))(crops_keys, crops_turns).reshape((PARCEL_DOWNWARD, PARCEL_ACROSS, VISITS_EACH_TILE, 1))
    decay = draw_decay(jax.random.fold_in(arg_keys[13], 71), 0)
    attn_gain = jnp.clip(1.0 + 0.18 * jax.random.normal(arg_keys[3], (D,), jnp.float32), 0.099609375, 1.8984375).astype(jnp.bfloat16)
    w_query = normal_values(arg_keys[4], (D, D), D ** -0.5, 0.15625)
    w_key = normal_values(arg_keys[5], (D, D), D ** -0.5, 0.15625)
    w_value = normal_values(arg_keys[6], (D, D), D ** -0.5, 0.15625)
    head_gain = jnp.clip(1.0 + 0.18 * jax.random.normal(arg_keys[7], (D,), jnp.float32), 0.099609375, 1.8984375).astype(jnp.bfloat16)
    w_out = normal_values(arg_keys[8], (D, D), D ** -0.5, 0.15625)
    moe_gain = jnp.clip(1.0 + 0.18 * jax.random.normal(arg_keys[9], (D,), jnp.float32), 0.099609375, 1.8984375).astype(jnp.bfloat16)
    w_gate = normal_values(arg_keys[10], (EXPERTS, D, FF), D ** -0.5, 0.15625, ((0, 4), (2, 8)))
    w_up = normal_values(arg_keys[11], (EXPERTS, D, FF), D ** -0.5, 0.15625, ((0, 4), (2, 8)))
    w_down = normal_values(arg_keys[12], (EXPERTS, FF, D), FF ** -0.5, 0.078125, ((0, 4), (1, 8)))
    return dict(x_spans=x_spans, crops=crops, decay=decay, attn_gain=attn_gain, w_query=w_query, w_key=w_key, w_value=w_value, head_gain=head_gain, w_out=w_out, moe_gain=moe_gain, w_gate=w_gate, w_up=w_up, w_down=w_down)


def rms_scale(values, width_eps):
    return lax.rsqrt(lax.optimization_barrier(jnp.mean(values * values, axis=-1, keepdims=True)) + width_eps)

def reference(x_spans, crops, decay, attn_gain, w_query, w_key, w_value, head_gain, w_out, moe_gain, w_gate, w_up, w_down):
    sequences = jnp.transpose(x_spans, (1, 2, 0, 3, 4)).reshape(PLOTS, VISITS_EACH_TILE, D)
    forgets = decay.reshape(PLOTS, VISITS_EACH_TILE, HEADS)

    def attend(packed):
        tokens, forget = packed
        widened = tokens.astype(jnp.float32)
        normed = (widened * rms_scale(widened, 1e-05) * attn_gain.astype(jnp.float32)).astype(jnp.bfloat16)
        query = jnp.dot(normed, w_query, preferred_element_type=jnp.float32).astype(jnp.bfloat16)
        key_vecs = jnp.dot(normed, w_key, preferred_element_type=jnp.float32).astype(jnp.bfloat16)
        value_vecs = jnp.dot(normed, w_value, preferred_element_type=jnp.float32).astype(jnp.bfloat16)
        query_heads = query.astype(jnp.float32).reshape(VISITS_EACH_TILE, HEADS, HEAD_DIM)
        key_heads = key_vecs.astype(jnp.float32).reshape(VISITS_EACH_TILE, HEADS, HEAD_DIM)
        value_heads = value_vecs.astype(jnp.float32).reshape(VISITS_EACH_TILE, HEADS, HEAD_DIM)
        cumulative = jnp.cumsum(forget, axis=0)
        scores = jnp.einsum('thd,shd->hts', query_heads, key_heads, precision=lax.Precision.HIGHEST)
        by_head = cumulative.T
        spread_vals = by_head[:, :, None] - by_head[:, None, :]
        causal = jnp.arange(VISITS_EACH_TILE)[:, None] >= jnp.arange(VISITS_EACH_TILE)[None, :]
        weights = jnp.exp(jnp.where(causal[None], spread_vals, -jnp.inf))
        mixed = jnp.einsum('hts,shd->thd', scores * weights, value_heads, precision=lax.Precision.HIGHEST)
        head_scale = head_gain.astype(jnp.float32).reshape(HEADS, HEAD_DIM)
        head_normed = (mixed * rms_scale(mixed, 1e-05) * head_scale).reshape(VISITS_EACH_TILE, D).astype(jnp.bfloat16)
        resid = (widened + jnp.dot(head_normed, w_out, preferred_element_type=jnp.float32)).astype(jnp.bfloat16)
        resid_wide = resid.astype(jnp.float32)
        routed = (resid_wide * rms_scale(resid_wide, 1e-05) * moe_gain.astype(jnp.float32)).astype(jnp.bfloat16)
        return (resid, routed)
    resid, routed = lax.map(attend, (sequences, forgets))
    crop_ids = crops.reshape(PLOTS, VISITS_EACH_TILE).astype(jnp.int32)
    onehot = (crop_ids[:, :, None] == jnp.arange(EXPERTS, dtype=jnp.int32)[None, None, :]).astype(jnp.int32)
    slot_ids = lax.optimization_barrier(jnp.sum((jnp.cumsum(onehot, axis=1) - onehot) * onehot, axis=-1)).astype(jnp.int32)
    plot_ids = jnp.broadcast_to(jnp.arange(PLOTS, dtype=jnp.int32)[:, None], (PLOTS, VISITS_EACH_TILE))
    buffer = jnp.zeros((EXPERTS, PLOTS, CAP, D), jnp.bfloat16).at[crop_ids, plot_ids, slot_ids].set(routed)

    def expert(operands):
        row_block, gate_matrix, up_matrix, down_matrix = operands
        flattened = row_block.reshape(PLOTS * CAP, D)
        gate_act = jnp.dot(flattened, gate_matrix, preferred_element_type=jnp.float32)
        up_act = jnp.dot(flattened, up_matrix, preferred_element_type=jnp.float32)
        hidden = (jax.nn.silu(gate_act) * up_act).astype(jnp.bfloat16)
        accumulated = jnp.zeros((PLOTS * CAP, D), jnp.float32)
        for group_index in range(N_DP):
            lower = group_index * HID_DEV
            partial_value = jnp.dot(hidden[:, lower:lower + HID_DEV], down_matrix[lower:lower + HID_DEV], preferred_element_type=jnp.float32).astype(jnp.bfloat16)
            partial_value = lax.optimization_barrier(partial_value)
            accumulated = accumulated + partial_value.astype(jnp.float32)
        return accumulated.astype(jnp.bfloat16).reshape(PLOTS, CAP, D)
    outputs = lax.map(expert, (buffer, w_gate, w_up, w_down))
    returned = outputs[crop_ids, plot_ids, slot_ids]
    layer_sum = (resid.astype(jnp.float32) + returned.astype(jnp.float32)).astype(jnp.bfloat16)
    return layer_sum.reshape(PARCEL_DOWNWARD, PARCEL_ACROSS, VISITS_EACH_TILE, D)
```

```python
import jax
import jax.numpy as jnp
from jax import lax
from jax.sharding import PartitionSpec as P

D = 1536
HEADS = 24
HEAD_DIM = 64
EXPERTS = 8
SPAN = 64


def rms_scale(values, width_eps):
    return lax.rsqrt(jnp.mean(values * values, axis=-1, keepdims=True) + width_eps)


def spread(buffers):
    return lax.all_gather(buffers, "dp", axis=0, tiled=True)


def deliver(buffers):
    return lax.all_to_all(buffers, "expert", split_axis=1, concat_axis=1, tiled=True)


def linear_mixing(query, key_vecs, value_vecs, forget, length):
    blocks = length // SPAN
    query_narrow = query.reshape(blocks, SPAN, HEADS, HEAD_DIM)
    key_narrow = key_vecs.reshape(blocks, SPAN, HEADS, HEAD_DIM)
    query_blocks = query_narrow.astype(jnp.float32)
    key_blocks = key_narrow.astype(jnp.float32)
    value_blocks = value_vecs.astype(jnp.float32).reshape(blocks, SPAN, HEADS, HEAD_DIM)
    within = jnp.cumsum(forget.reshape(blocks, SPAN, HEADS), axis=1)
    block_total = within[:, -1, :]
    scores = jnp.einsum(
        "nthd,nshd->nhts", query_narrow, key_narrow, preferred_element_type=jnp.float32
    )
    by_head = jnp.transpose(within, (0, 2, 1))
    spread_vals = by_head[:, :, :, None] - by_head[:, :, None, :]
    causal = jnp.arange(SPAN)[:, None] >= jnp.arange(SPAN)[None, :]
    weights = jnp.exp(jnp.where(causal[None, None], spread_vals, -jnp.inf))
    local_part = jnp.einsum(
        "nhts,nshd->nthd", scores * weights, value_blocks, precision=lax.Precision.HIGHEST
    )
    carried_keys = key_blocks * jnp.exp(block_total[:, None, :] - within)[..., None]
    block_states = jnp.einsum(
        "nshd,nshe->nhde", carried_keys, value_blocks, precision=lax.Precision.HIGHEST
    )

    def advance(carried, element):
        block_state, total_now = element
        return (carried * jnp.exp(total_now)[:, None, None] + block_state, carried)

    _, entering = lax.scan(
        advance, jnp.zeros((HEADS, HEAD_DIM, HEAD_DIM), jnp.float32), (block_states, block_total)
    )
    earlier_part = jnp.einsum(
        "nthd,nhde->nthe",
        query_blocks * jnp.exp(within)[..., None],
        entering,
        precision=lax.Precision.HIGHEST,
    )
    return (local_part + earlier_part).reshape(length, HEADS, HEAD_DIM)


def on_device(
    x_spans,
    crops,
    decay,
    attn_gain,
    w_query,
    w_key,
    w_value,
    head_gain,
    w_out,
    moe_gain,
    w_gate,
    w_up,
    w_down,
):
    arrived = lax.all_to_all(x_spans, "dp", split_axis=1, concat_axis=0, tiled=True)
    length = arrived.shape[0] * arrived.shape[3]
    tokens = arrived.reshape(length, D)
    forget = decay.reshape(length, HEADS)
    widened = tokens.astype(jnp.float32)
    normed = (widened * rms_scale(widened, 1e-05) * attn_gain.astype(jnp.float32)).astype(
        jnp.bfloat16
    )
    query = jnp.dot(normed, w_query, preferred_element_type=jnp.float32).astype(jnp.bfloat16)
    key_vecs = jnp.dot(normed, w_key, preferred_element_type=jnp.float32).astype(jnp.bfloat16)
    value_vecs = jnp.dot(normed, w_value, preferred_element_type=jnp.float32).astype(jnp.bfloat16)
    mixed = linear_mixing(query, key_vecs, value_vecs, forget, length)
    head_scale = head_gain.astype(jnp.float32).reshape(HEADS, HEAD_DIM)
    head_normed = (
        (mixed * rms_scale(mixed, 1e-05) * head_scale).reshape(length, D).astype(jnp.bfloat16)
    )
    resid = (widened + jnp.dot(head_normed, w_out, preferred_element_type=jnp.float32)).astype(
        jnp.bfloat16
    )
    resid_wide = resid.astype(jnp.float32)
    routed = (resid_wide * rms_scale(resid_wide, 1e-05) * moe_gain.astype(jnp.float32)).astype(
        jnp.bfloat16
    )
    crop_ids = crops.reshape(length)
    onehot = (crop_ids[:, None] == jnp.arange(EXPERTS, dtype=jnp.int32)[None, :]).astype(jnp.int32)
    slot_ids = jnp.sum((jnp.cumsum(onehot, axis=0) - onehot) * onehot, axis=1)
    capacity = length // 4
    position = crop_ids * capacity + slot_ids
    select = (jnp.arange(EXPERTS * capacity, dtype=jnp.int32)[:, None] == position[None, :]).astype(
        jnp.bfloat16
    )
    packed = jnp.dot(select, routed, preferred_element_type=jnp.float32).astype(jnp.bfloat16)
    owners = lax.axis_size("expert")
    local_count = w_gate.shape[0]
    outgoing = packed.reshape(1, owners, EXPERTS * capacity // owners, D)
    gathered = spread(deliver(outgoing))
    sources = gathered.shape[0]
    grouped = gathered.reshape(sources, owners, local_count, capacity, D)
    gate_act = jnp.einsum("sojcd,jdf->sojcf", grouped, w_gate, preferred_element_type=jnp.float32)
    up_act = jnp.einsum("sojcd,jdf->sojcf", grouped, w_up, preferred_element_type=jnp.float32)
    hidden = (jax.nn.silu(gate_act) * up_act).astype(jnp.bfloat16)
    term = jnp.einsum("sojcf,jfd->sojcd", hidden, w_down, preferred_element_type=jnp.float32)
    summed = lax.psum_scatter(
        term.reshape(1 * lax.axis_size("dp"), owners, local_count * capacity, D).astype(
            jnp.bfloat16
        ),
        "dp",
        scatter_dimension=0,
        tiled=True,
    )
    own_sums = summed[0]
    returned = lax.all_to_all(own_sums, "expert", split_axis=0, concat_axis=0, tiled=True)
    flat_back = returned.reshape(EXPERTS * capacity, D)
    expert_out = jnp.einsum("pl,pd->ld", select, flat_back, preferred_element_type=jnp.float32)
    layer_sum = (resid_wide + expert_out).astype(jnp.bfloat16)
    return layer_sum.reshape(1, 1, length, D)


def solution(mesh):
    return jax.shard_map(
        on_device,
        mesh=mesh,
        in_specs=(
            P("dp", None, "expert", None, None),
            P("dp", "expert", None, None),
            P("dp", "expert", None, None),
            P(),
            P(),
            P(),
            P(),
            P(),
            P(),
            P(),
            P("expert", None, "dp"),
            P("expert", None, "dp"),
            P("expert", "dp", None),
        ),
        out_specs=P("dp", "expert", None, None),
        check_vma=False,
    )
```

```python
import jax
import jax.numpy as jnp
from jax import lax
from jax.experimental import pallas as pl
from jax.experimental.pallas import tpu as pltpu
from jax.sharding import PartitionSpec as P

D = 1536
HEADS = 24
HEAD_DIM = 64
EXPERTS = 8
SPAN = 64
NZ = 4
NX = 2
NY = 2
NC = 2
CHIPS = NZ * NX * NY
Z_UP, Z_DOWN, BY_X, BY_Y, CORE = range(5)


def place():
    dp, expert = lax.axis_index("dp"), lax.axis_index("expert")
    return dp // NX, dp % NX, expert // NC, expert % NC


def device(z, x, y, c):
    return (z * NX + x, y * NC + c)


def plot_of(z, x, y, c):
    return (z * NX + x) * (NY * NC) + y * NC + c


def chip_of(z, x, y):
    return (z * NX + x) * NY + y


def partner(kind, z, x, y, c):
    if kind == Z_UP:
        return device(z + 1, x, y, c)
    if kind == Z_DOWN:
        return device(z - 1, x, y, c)
    if kind == BY_X:
        return device(z, 1 - x, y, c)
    if kind == BY_Y:
        return device(z, x, 1 - y, c)
    return device(z, x, y, 1 - c)


def only_if(condition, body):
    if condition is None:
        body()
    else:
        pl.when(condition)(body)


def exists(kind, z):
    return {Z_UP: z < NZ - 1, Z_DOWN: z > 0}.get(kind)


def greet(z, x, y, c):
    barrier = pltpu.get_barrier_semaphore()
    for kind in range(5):

        def signal(kind=kind):
            pl.semaphore_signal(
                barrier,
                inc=1,
                device_id=partner(kind, z, x, y, c),
                device_id_type=pl.DeviceIdType.MESH,
            )

        only_if(exists(kind, z), signal)
    pl.semaphore_wait(barrier, 3 + jnp.where(z > 0, 1, 0) + jnp.where(z < NZ - 1, 1, 0))


def gather_kernel(own_ref, out_ref, send_sem, recv_sem, core_sem, local_sem):
    z, x, y, c = place()
    half = own_ref.shape[0] // 2
    greet(z, x, y, c)
    sent = []

    def rows(h):
        return pl.ds(h * half, half)

    def copy(h, kind, bz, bx, by, own):
        chip = chip_of(bz, bx, by)
        target = out_ref.at[plot_of(bz, bx, by, c), rows(h)]
        return pltpu.make_async_remote_copy(
            src_ref=own_ref.at[rows(h)] if own else target,
            dst_ref=target,
            send_sem=send_sem.at[h, kind, chip],
            recv_sem=(core_sem if kind == CORE else recv_sem).at[h, chip],
            device_id=partner(kind, z, x, y, c),
            device_id_type=pl.DeviceIdType.MESH,
        )

    def send(h, kind, bz, bx, by, guard, own=False):
        def both(action):
            def body():
                def inner():
                    action(copy(h, kind, bz, bx, by, own))

                only_if(exists(kind, z), inner)

            only_if(guard, body)

        both(lambda made: made.start())
        sent.append(lambda: both(lambda made: made.wait_send()))

    def arrive(h, bz, bx, by, guard):
        only_if(guard, lambda: copy(h, BY_X, bz, bx, by, False).wait_recv())

    stay = pltpu.make_async_copy(own_ref, out_ref.at[plot_of(z, x, y, c)], local_sem)
    stay.start()
    middle = (BY_X, BY_Y)
    last = (BY_Y, BY_X)
    for h in range(2):
        for kind in (Z_UP, Z_DOWN, middle[h], last[h], CORE):
            send(h, kind, z, x, y, None, own=True)

    def spots(step):
        if step == 0:
            return [(z, None, None)]
        return [(z - step, z - step >= 0, Z_UP), (z + step, z + step < NZ, Z_DOWN)]

    for turn in range(NZ + 2):
        if 1 <= turn < NZ:
            for bz, guard, way in spots(turn):
                for h in range(2):
                    arrive(h, bz, x, y, guard)
                    for kind in (way, middle[h], last[h], CORE):
                        send(h, kind, bz, x, y, guard)
        if 0 <= turn - 1 < NZ:
            for bz, guard, _ in spots(turn - 1):
                for h in range(2):
                    bx, by = (1 - x, y) if h == 0 else (x, 1 - y)
                    arrive(h, bz, bx, by, guard)
                    for kind in (last[h], CORE):
                        send(h, kind, bz, bx, by, guard)
        if 0 <= turn - 2 < NZ:
            for bz, guard, _ in spots(turn - 2):
                for h in range(2):
                    for bx, by in ((x, 1 - y), (1 - x, 1 - y)) if h == 0 else ((1 - x, y), (1 - x, 1 - y)):
                        arrive(h, bz, bx, by, guard)
                        send(h, CORE, bz, bx, by, guard)
    for chip in range(CHIPS):
        bz, bx, by = chip // (NX * NY), chip // NY % NX, chip % NY
        for h in range(2):
            landed = out_ref.at[plot_of(bz, bx, by, 1 - c), rows(h)]
            pltpu.make_async_remote_copy(
                src_ref=landed,
                dst_ref=landed,
                send_sem=send_sem.at[h, CORE, chip],
                recv_sem=core_sem.at[h, chip],
                device_id=partner(CORE, z, x, y, c),
                device_id_type=pl.DeviceIdType.MESH,
            ).wait_recv()
    for wait in sent:
        wait()
    stay.wait()


def gather_plots(own):
    length = own.shape[0]
    plots = CHIPS * NC
    return pl.pallas_call(
        gather_kernel,
        out_shape=jax.ShapeDtypeStruct((plots, length, D), jnp.bfloat16),
        in_specs=[pl.BlockSpec(memory_space=pltpu.VMEM)],
        out_specs=pl.BlockSpec(memory_space=pl.ANY),
        scratch_shapes=[
            pltpu.SemaphoreType.DMA((2, 5, CHIPS)),
            pltpu.SemaphoreType.DMA((2, CHIPS)),
            pltpu.SemaphoreType.DMA((2, CHIPS)),
            pltpu.SemaphoreType.DMA,
        ],
        compiler_params=pltpu.CompilerParams(collective_id=0, has_side_effects=True),
    )(own)


def reduce_kernel(
    terms_ref,
    out_ref,
    core_buf,
    first_buf,
    second_buf,
    up_buf,
    down_buf,
    core_sem,
    first_sem,
    second_sem,
    up_sem,
    down_sem,
):
    z, x, y, c = place()
    half = out_ref.shape[0] // 2
    greet(z, x, y, c)
    sent = []

    def rows(h):
        return pl.ds(h * half, half)

    def move(src, buf, sem, index, kind):
        return pltpu.make_async_remote_copy(
            src_ref=src,
            dst_ref=buf.at[index],
            send_sem=sem.at[(0, *index)],
            recv_sem=sem.at[(1, *index)],
            device_id=partner(kind, z, x, y, c),
            device_id_type=pl.DeviceIdType.MESH,
        )

    def send(src, buf, sem, index, kind, guard=None):
        only_if(guard, lambda: move(src, buf, sem, index, kind).start())
        sent.append(lambda: only_if(guard, lambda: move(src, buf, sem, index, kind).wait_send()))

    def arrive(buf, sem, index, kind):
        move(buf.at[index], buf, sem, index, kind).wait_recv()

    def wide(ref, *index):
        return ref[index].astype(jnp.float32)

    low = jnp.where(z < NZ // 2, 1, 0)

    def layer(turn):
        return low * (NZ - 1 - turn) + (1 - low) * turn

    def spot(h, first_other, second_other):
        first, second = (y, x) if h == 0 else (x, y)
        first = 1 - first if first_other else first
        second = 1 - second if second_other else second
        return (second, first) if h == 0 else (first, second)

    order = ((1, 1), (1, 0), (0, 1), (0, 0))
    first_kind, second_kind = (BY_Y, BY_X), (BY_X, BY_Y)
    for turn in range(NZ):
        for first_other, second_other in order:
            for h in range(2):
                bx, by = spot(h, first_other, second_other)
                bz = layer(turn)
                send(
                    terms_ref.at[plot_of(bz, bx, by, 1 - c), rows(h)],
                    core_buf,
                    core_sem,
                    (h, chip_of(bz, bx, by)),
                    CORE,
                )

    def pair(turn):
        bz = layer(turn)
        for first_other, second_other in order:
            for h in range(2):
                bx, by = spot(h, first_other, second_other)
                index = (h, chip_of(bz, bx, by))
                arrive(core_buf, core_sem, index, CORE)
                total = wide(core_buf, *index) + wide(
                    terms_ref, plot_of(bz, bx, by, c), rows(h)
                )
                core_buf[index] = total.astype(jnp.bfloat16)
                if first_other:
                    second = bx if h == 0 else by
                    send(
                        core_buf.at[index], first_buf, first_sem, (h, bz, second), first_kind[h]
                    )

    def across(turn):
        bz = layer(turn)
        for h in range(2):
            bx, by = spot(h, 0, 1)
            index = (h, bz, bx if h == 0 else by)
            arrive(first_buf, first_sem, index, first_kind[h])
            total = wide(first_buf, *index) + wide(core_buf, h, chip_of(bz, bx, by))
            first_buf[index] = total.astype(jnp.bfloat16)
            send(first_buf.at[index], second_buf, second_sem, (h, bz), second_kind[h])

    def along(turn):
        bz = layer(turn)
        for h in range(2):
            bx, by = spot(h, 0, 0)
            index = (h, bz, bx if h == 0 else by)
            arrive(first_buf, first_sem, index, first_kind[h])
            arrive(second_buf, second_sem, (h, bz), second_kind[h])
            total = (
                wide(first_buf, *index)
                + wide(core_buf, h, chip_of(bz, bx, by))
                + wide(second_buf, h, bz)
            )
            for buf, sem, kind, goes, comes in (
                (up_buf, up_sem, Z_UP, bz > z, z > 0),
                (down_buf, down_sem, Z_DOWN, bz < z, z < NZ - 1),
            ):

                @pl.when(goes)
                def _():
                    @pl.when(comes)
                    def _():
                        arrive(buf, sem, (h, bz), kind)
                        buf[h, bz] = (total + wide(buf, h, bz)).astype(jnp.bfloat16)

                    @pl.when(jnp.logical_not(comes))
                    def _():
                        buf[h, bz] = total.astype(jnp.bfloat16)

                send(buf.at[h, bz], buf, sem, (h, bz), kind, goes)

    for turn in range(NZ + 2):
        if turn < NZ:
            pair(turn)
        if 0 <= turn - 1 < NZ:
            across(turn - 1)
        if 0 <= turn - 2 < NZ:
            along(turn - 2)
    for h in range(2):
        mine = x if h == 0 else y
        total = (
            wide(first_buf, h, z, mine)
            + wide(core_buf, h, chip_of(z, x, y))
            + wide(second_buf, h, z)
        )

        @pl.when(z == 0)
        def _():
            arrive(down_buf, down_sem, (h, z), Z_DOWN)
            out_ref[rows(h)] = (total + wide(down_buf, h, z)).astype(jnp.bfloat16)

        @pl.when(z == NZ - 1)
        def _():
            arrive(up_buf, up_sem, (h, z), Z_UP)
            out_ref[rows(h)] = (total + wide(up_buf, h, z)).astype(jnp.bfloat16)

        @pl.when(jnp.logical_and(z > 0, z < NZ - 1))
        def _():
            arrive(down_buf, down_sem, (h, z), Z_DOWN)
            arrive(up_buf, up_sem, (h, z), Z_UP)
            both = wide(up_buf, h, z) + wide(down_buf, h, z)
            out_ref[rows(h)] = (total + both).astype(jnp.bfloat16)

    for wait in sent:
        wait()


def reduce_plots(terms):
    length = terms.shape[1]
    half = length // 2

    def blocks(*lead):
        return pltpu.VMEM((*lead, half, D), jnp.bfloat16)

    return pl.pallas_call(
        reduce_kernel,
        out_shape=jax.ShapeDtypeStruct((length, D), jnp.bfloat16),
        in_specs=[pl.BlockSpec(memory_space=pltpu.VMEM)],
        out_specs=pl.BlockSpec(memory_space=pltpu.VMEM),
        scratch_shapes=[
            blocks(2, CHIPS),
            blocks(2, NZ, 2),
            blocks(2, NZ),
            blocks(2, NZ),
            blocks(2, NZ),
            pltpu.SemaphoreType.DMA((2, 2, CHIPS)),
            pltpu.SemaphoreType.DMA((2, 2, NZ, 2)),
            pltpu.SemaphoreType.DMA((2, 2, NZ)),
            pltpu.SemaphoreType.DMA((2, 2, NZ)),
            pltpu.SemaphoreType.DMA((2, 2, NZ)),
        ],
        compiler_params=pltpu.CompilerParams(
            collective_id=1, has_side_effects=True, vmem_limit_bytes=48 * 1024 * 1024
        ),
    )(terms)


def slot_positions(crop_ids, capacity):
    length = crop_ids.shape[0]
    same = crop_ids[:, None] == crop_ids[None, :]
    earlier = jnp.arange(length)[None, :] < jnp.arange(length)[:, None]
    slot_ids = jnp.sum(jnp.logical_and(same, earlier).astype(jnp.int32), axis=1)
    return crop_ids * capacity + slot_ids


def routed_experts(routed, crop_ids, w_gate, w_up, w_down):
    length = routed.shape[0]
    capacity = length // 4
    plots = CHIPS * NC
    local_count = w_gate.shape[0]
    position = slot_positions(crop_ids, capacity)
    everywhere = lax.all_gather(position, ("dp", "expert"), axis=0)
    tokens = gather_plots(routed)
    held = local_count * capacity
    slots = lax.axis_index("expert") * held + jnp.arange(held, dtype=jnp.int32)
    select = (everywhere[:, None, :] == slots[None, :, None]).astype(jnp.bfloat16)
    select = select.reshape(plots, local_count, capacity, length)
    packed = jnp.einsum(
        "pjct,ptd->jpcd", select, tokens, preferred_element_type=jnp.float32
    ).astype(jnp.bfloat16)
    packed = packed.reshape(local_count, plots * capacity, D)
    gate_act = jnp.einsum("jrd,jdf->jrf", packed, w_gate, preferred_element_type=jnp.float32)
    up_act = jnp.einsum("jrd,jdf->jrf", packed, w_up, preferred_element_type=jnp.float32)
    hidden = (jax.nn.silu(gate_act) * up_act).astype(jnp.bfloat16)
    term = jnp.einsum("jrf,jfd->jrd", hidden, w_down, preferred_element_type=jnp.float32)
    term = term.astype(jnp.bfloat16).reshape(local_count, plots, capacity, D)
    by_token = jnp.einsum(
        "pjct,jpcd->ptd", select, term, preferred_element_type=jnp.float32
    ).astype(jnp.bfloat16)
    return reduce_plots(by_token)


def rms_scale(values, width_eps):
    return lax.rsqrt(jnp.mean(values * values, axis=-1, keepdims=True) + width_eps)


def spread(buffers):
    return lax.all_gather(buffers, "dp", axis=0, tiled=True)


def deliver(buffers):
    return lax.all_to_all(buffers, "expert", split_axis=1, concat_axis=1, tiled=True)


def linear_mixing(query, key_vecs, value_vecs, forget, length):
    blocks = length // SPAN
    query_narrow = query.reshape(blocks, SPAN, HEADS, HEAD_DIM)
    key_narrow = key_vecs.reshape(blocks, SPAN, HEADS, HEAD_DIM)
    query_blocks = query_narrow.astype(jnp.float32)
    key_blocks = key_narrow.astype(jnp.float32)
    value_blocks = value_vecs.astype(jnp.float32).reshape(blocks, SPAN, HEADS, HEAD_DIM)
    within = jnp.cumsum(forget.reshape(blocks, SPAN, HEADS), axis=1)
    block_total = within[:, -1, :]
    scores = jnp.einsum(
        "nthd,nshd->nhts", query_narrow, key_narrow, preferred_element_type=jnp.float32
    )
    by_head = jnp.transpose(within, (0, 2, 1))
    spread_vals = by_head[:, :, :, None] - by_head[:, :, None, :]
    causal = jnp.arange(SPAN)[:, None] >= jnp.arange(SPAN)[None, :]
    weights = jnp.exp(jnp.where(causal[None, None], spread_vals, -jnp.inf))
    local_part = jnp.einsum(
        "nhts,nshd->nthd", scores * weights, value_blocks, precision=lax.Precision.HIGHEST
    )
    carried_keys = key_blocks * jnp.exp(block_total[:, None, :] - within)[..., None]
    block_states = jnp.einsum(
        "nshd,nshe->nhde", carried_keys, value_blocks, precision=lax.Precision.HIGHEST
    )

    def advance(carried, element):
        block_state, total_now = element
        return (carried * jnp.exp(total_now)[:, None, None] + block_state, carried)

    _, entering = lax.scan(
        advance, jnp.zeros((HEADS, HEAD_DIM, HEAD_DIM), jnp.float32), (block_states, block_total)
    )
    earlier_part = jnp.einsum(
        "nthd,nhde->nthe",
        query_blocks * jnp.exp(within)[..., None],
        entering,
        precision=lax.Precision.HIGHEST,
    )
    return (local_part + earlier_part).reshape(length, HEADS, HEAD_DIM)


def on_device(
    x_spans,
    crops,
    decay,
    attn_gain,
    w_query,
    w_key,
    w_value,
    head_gain,
    w_out,
    moe_gain,
    w_gate,
    w_up,
    w_down,
):
    arrived = lax.all_to_all(x_spans, "dp", split_axis=1, concat_axis=0, tiled=True)
    length = arrived.shape[0] * arrived.shape[3]
    tokens = arrived.reshape(length, D)
    forget = decay.reshape(length, HEADS)
    widened = tokens.astype(jnp.float32)
    normed = (widened * rms_scale(widened, 1e-05) * attn_gain.astype(jnp.float32)).astype(
        jnp.bfloat16
    )
    query = jnp.dot(normed, w_query, preferred_element_type=jnp.float32).astype(jnp.bfloat16)
    key_vecs = jnp.dot(normed, w_key, preferred_element_type=jnp.float32).astype(jnp.bfloat16)
    value_vecs = jnp.dot(normed, w_value, preferred_element_type=jnp.float32).astype(jnp.bfloat16)
    mixed = linear_mixing(query, key_vecs, value_vecs, forget, length)
    head_scale = head_gain.astype(jnp.float32).reshape(HEADS, HEAD_DIM)
    head_normed = (
        (mixed * rms_scale(mixed, 1e-05) * head_scale).reshape(length, D).astype(jnp.bfloat16)
    )
    resid = (widened + jnp.dot(head_normed, w_out, preferred_element_type=jnp.float32)).astype(
        jnp.bfloat16
    )
    resid_wide = resid.astype(jnp.float32)
    routed = (resid_wide * rms_scale(resid_wide, 1e-05) * moe_gain.astype(jnp.float32)).astype(
        jnp.bfloat16
    )
    crop_ids = crops.reshape(length)
    if lax.axis_size("dp") == NZ * NX and lax.axis_size("expert") == NY * NC:
        expert_out = routed_experts(routed, crop_ids, w_gate, w_up, w_down)
        layer_sum = (resid_wide + expert_out.astype(jnp.float32)).astype(jnp.bfloat16)
        return layer_sum.reshape(1, 1, length, D)
    onehot = (crop_ids[:, None] == jnp.arange(EXPERTS, dtype=jnp.int32)[None, :]).astype(jnp.int32)
    slot_ids = jnp.sum((jnp.cumsum(onehot, axis=0) - onehot) * onehot, axis=1)
    capacity = length // 4
    position = crop_ids * capacity + slot_ids
    select = (jnp.arange(EXPERTS * capacity, dtype=jnp.int32)[:, None] == position[None, :]).astype(
        jnp.bfloat16
    )
    packed = jnp.dot(select, routed, preferred_element_type=jnp.float32).astype(jnp.bfloat16)
    owners = lax.axis_size("expert")
    local_count = w_gate.shape[0]
    outgoing = packed.reshape(1, owners, EXPERTS * capacity // owners, D)
    gathered = spread(deliver(outgoing))
    sources = gathered.shape[0]
    grouped = gathered.reshape(sources, owners, local_count, capacity, D)
    gate_act = jnp.einsum("sojcd,jdf->sojcf", grouped, w_gate, preferred_element_type=jnp.float32)
    up_act = jnp.einsum("sojcd,jdf->sojcf", grouped, w_up, preferred_element_type=jnp.float32)
    hidden = (jax.nn.silu(gate_act) * up_act).astype(jnp.bfloat16)
    term = jnp.einsum("sojcf,jfd->sojcd", hidden, w_down, preferred_element_type=jnp.float32)
    summed = lax.psum_scatter(
        term.reshape(1 * lax.axis_size("dp"), owners, local_count * capacity, D).astype(
            jnp.bfloat16
        ),
        "dp",
        scatter_dimension=0,
        tiled=True,
    )
    own_sums = summed[0]
    returned = lax.all_to_all(own_sums, "expert", split_axis=0, concat_axis=0, tiled=True)
    flat_back = returned.reshape(EXPERTS * capacity, D)
    expert_out = jnp.einsum("pl,pd->ld", select, flat_back, preferred_element_type=jnp.float32)
    layer_sum = (resid_wide + expert_out).astype(jnp.bfloat16)
    return layer_sum.reshape(1, 1, length, D)


def solution(mesh):
    return jax.shard_map(
        on_device,
        mesh=mesh,
        in_specs=(
            P("dp", None, "expert", None, None),
            P("dp", "expert", None, None),
            P("dp", "expert", None, None),
            P(),
            P(),
            P(),
            P(),
            P(),
            P(),
            P(),
            P("expert", None, "dp"),
            P("expert", None, "dp"),
            P("expert", "dp", None),
        ),
        out_specs=P("dp", "expert", None, None),
        check_vma=False,
    )
```

```python
import jax
import jax.numpy as jnp
from jax import lax
from jax.experimental import pallas as pl
from jax.experimental.pallas import tpu as pltpu
from jax.sharding import PartitionSpec as P

D = 1536
HEADS = 24
HEAD_DIM = 64
EXPERTS = 8
EXTRA = 16
NZ = 4
NX = 2
NY = 2
NC = 2
CHIPS = NZ * NX * NY
Z_UP, Z_DOWN, BY_X, BY_Y, CORE = range(5)


def place():
    dp, expert = lax.axis_index("dp"), lax.axis_index("expert")
    return dp // NX, dp % NX, expert // NC, expert % NC


def device(z, x, y, c):
    return (z * NX + x, y * NC + c)


def plot_of(z, x, y, c):
    return (z * NX + x) * (NY * NC) + y * NC + c


def chip_of(z, x, y):
    return (z * NX + x) * NY + y


def partner(kind, z, x, y, c):
    if kind == Z_UP:
        return device(z + 1, x, y, c)
    if kind == Z_DOWN:
        return device(z - 1, x, y, c)
    if kind == BY_X:
        return device(z, 1 - x, y, c)
    if kind == BY_Y:
        return device(z, x, 1 - y, c)
    return device(z, x, y, 1 - c)


def only_if(condition, body):
    if condition is None:
        body()
    else:
        pl.when(condition)(body)


def exists(kind, z):
    return {Z_UP: z < NZ - 1, Z_DOWN: z > 0}.get(kind)


def greet(z, x, y, c):
    barrier = pltpu.get_barrier_semaphore()
    for kind in range(5):

        def signal(kind=kind):
            pl.semaphore_signal(
                barrier,
                inc=1,
                device_id=partner(kind, z, x, y, c),
                device_id_type=pl.DeviceIdType.MESH,
            )

        only_if(exists(kind, z), signal)
    pl.semaphore_wait(barrier, 3 + jnp.where(z > 0, 1, 0) + jnp.where(z < NZ - 1, 1, 0))


def gather_kernel(own_ref, out_ref, send_sem, recv_sem, core_sem, local_sem):
    z, x, y, c = place()
    length = own_ref.shape[0]
    half = length // (2 * EXTRA) * EXTRA
    greet(z, x, y, c)
    sent = []

    def rows(h):
        return pl.ds(h * half, half if h == 0 else length - half)

    def copy(h, kind, bz, bx, by, own):
        chip = chip_of(bz, bx, by)
        target = out_ref.at[plot_of(bz, bx, by, c), rows(h)]
        return pltpu.make_async_remote_copy(
            src_ref=own_ref.at[rows(h)] if own else target,
            dst_ref=target,
            send_sem=send_sem.at[h, kind, chip],
            recv_sem=(core_sem if kind == CORE else recv_sem).at[h, chip],
            device_id=partner(kind, z, x, y, c),
            device_id_type=pl.DeviceIdType.MESH,
        )

    def send(h, kind, bz, bx, by, guard, own=False):
        def both(action):
            def body():
                def inner():
                    action(copy(h, kind, bz, bx, by, own))

                only_if(exists(kind, z), inner)

            only_if(guard, body)

        both(lambda made: made.start())
        sent.append(lambda: both(lambda made: made.wait_send()))

    def arrive(h, bz, bx, by, guard):
        only_if(guard, lambda: copy(h, BY_X, bz, bx, by, False).wait_recv())

    stay = pltpu.make_async_copy(own_ref, out_ref.at[plot_of(z, x, y, c)], local_sem)
    stay.start()
    middle = (BY_X, BY_Y)
    last = (BY_Y, BY_X)
    for h in range(2):
        for kind in (Z_UP, Z_DOWN, middle[h], last[h], CORE):
            send(h, kind, z, x, y, None, own=True)

    def spots(step):
        if step == 0:
            return [(z, None, None)]
        return [(z - step, z - step >= 0, Z_UP), (z + step, z + step < NZ, Z_DOWN)]

    for turn in range(NZ + 2):
        if 1 <= turn < NZ:
            for bz, guard, way in spots(turn):
                for h in range(2):
                    arrive(h, bz, x, y, guard)
                    for kind in (way, middle[h], last[h], CORE):
                        send(h, kind, bz, x, y, guard)
        if 0 <= turn - 1 < NZ:
            for bz, guard, _ in spots(turn - 1):
                for h in range(2):
                    bx, by = (1 - x, y) if h == 0 else (x, 1 - y)
                    arrive(h, bz, bx, by, guard)
                    for kind in (last[h], CORE):
                        send(h, kind, bz, bx, by, guard)
        if 0 <= turn - 2 < NZ:
            for bz, guard, _ in spots(turn - 2):
                for h in range(2):
                    for bx, by in ((x, 1 - y), (1 - x, 1 - y)) if h == 0 else ((1 - x, y), (1 - x, 1 - y)):
                        arrive(h, bz, bx, by, guard)
                        send(h, CORE, bz, bx, by, guard)
    for chip in range(CHIPS):
        bz, bx, by = chip // (NX * NY), chip // NY % NX, chip % NY
        for h in range(2):
            landed = out_ref.at[plot_of(bz, bx, by, 1 - c), rows(h)]
            pltpu.make_async_remote_copy(
                src_ref=landed,
                dst_ref=landed,
                send_sem=send_sem.at[h, CORE, chip],
                recv_sem=core_sem.at[h, chip],
                device_id=partner(CORE, z, x, y, c),
                device_id_type=pl.DeviceIdType.MESH,
            ).wait_recv()
    for wait in sent:
        wait()
    stay.wait()


def gather_plots(own):
    length = own.shape[0]
    plots = CHIPS * NC
    return pl.pallas_call(
        gather_kernel,
        out_shape=jax.ShapeDtypeStruct((plots, length, D), jnp.bfloat16),
        in_specs=[pl.BlockSpec(memory_space=pltpu.VMEM)],
        out_specs=pl.BlockSpec(memory_space=pl.ANY),
        scratch_shapes=[
            pltpu.SemaphoreType.DMA((2, 5, CHIPS)),
            pltpu.SemaphoreType.DMA((2, CHIPS)),
            pltpu.SemaphoreType.DMA((2, CHIPS)),
            pltpu.SemaphoreType.DMA,
        ],
        compiler_params=pltpu.CompilerParams(collective_id=0, has_side_effects=True),
    )(own)


def reduce_kernel(
    terms_ref,
    out_ref,
    core_buf,
    first_buf,
    second_buf,
    up_buf,
    down_buf,
    core_sem,
    first_sem,
    second_sem,
    up_sem,
    down_sem,
):
    z, x, y, c = place()
    half = out_ref.shape[0] // 2
    greet(z, x, y, c)
    sent = []

    def rows(h):
        return pl.ds(h * half, half)

    def move(src, buf, sem, index, kind):
        return pltpu.make_async_remote_copy(
            src_ref=src,
            dst_ref=buf.at[index],
            send_sem=sem.at[(0, *index)],
            recv_sem=sem.at[(1, *index)],
            device_id=partner(kind, z, x, y, c),
            device_id_type=pl.DeviceIdType.MESH,
        )

    def send(src, buf, sem, index, kind, guard=None):
        only_if(guard, lambda: move(src, buf, sem, index, kind).start())
        sent.append(lambda: only_if(guard, lambda: move(src, buf, sem, index, kind).wait_send()))

    def arrive(buf, sem, index, kind):
        move(buf.at[index], buf, sem, index, kind).wait_recv()

    def wide(ref, *index):
        return ref[index].astype(jnp.float32)

    low = jnp.where(z < NZ // 2, 1, 0)

    def layer(turn):
        return low * (NZ - 1 - turn) + (1 - low) * turn

    def spot(h, first_other, second_other):
        first, second = (y, x) if h == 0 else (x, y)
        first = 1 - first if first_other else first
        second = 1 - second if second_other else second
        return (second, first) if h == 0 else (first, second)

    order = ((1, 1), (1, 0), (0, 1), (0, 0))
    first_kind, second_kind = (BY_Y, BY_X), (BY_X, BY_Y)
    for turn in range(NZ):
        for first_other, second_other in order:
            for h in range(2):
                bx, by = spot(h, first_other, second_other)
                bz = layer(turn)
                send(
                    terms_ref.at[plot_of(bz, bx, by, 1 - c), rows(h)],
                    core_buf,
                    core_sem,
                    (h, chip_of(bz, bx, by)),
                    CORE,
                )

    def pair(turn):
        bz = layer(turn)
        for first_other, second_other in order:
            for h in range(2):
                bx, by = spot(h, first_other, second_other)
                index = (h, chip_of(bz, bx, by))
                arrive(core_buf, core_sem, index, CORE)
                total = wide(core_buf, *index) + wide(
                    terms_ref, plot_of(bz, bx, by, c), rows(h)
                )
                core_buf[index] = total.astype(jnp.bfloat16)
                if first_other:
                    second = bx if h == 0 else by
                    send(
                        core_buf.at[index], first_buf, first_sem, (h, bz, second), first_kind[h]
                    )

    def across(turn):
        bz = layer(turn)
        for h in range(2):
            bx, by = spot(h, 0, 1)
            index = (h, bz, bx if h == 0 else by)
            arrive(first_buf, first_sem, index, first_kind[h])
            total = wide(first_buf, *index) + wide(core_buf, h, chip_of(bz, bx, by))
            first_buf[index] = total.astype(jnp.bfloat16)
            send(first_buf.at[index], second_buf, second_sem, (h, bz), second_kind[h])

    def along(turn):
        bz = layer(turn)
        for h in range(2):
            bx, by = spot(h, 0, 0)
            index = (h, bz, bx if h == 0 else by)
            arrive(first_buf, first_sem, index, first_kind[h])
            arrive(second_buf, second_sem, (h, bz), second_kind[h])
            total = (
                wide(first_buf, *index)
                + wide(core_buf, h, chip_of(bz, bx, by))
                + wide(second_buf, h, bz)
            )
            for buf, sem, kind, goes, comes in (
                (up_buf, up_sem, Z_UP, bz > z, z > 0),
                (down_buf, down_sem, Z_DOWN, bz < z, z < NZ - 1),
            ):

                @pl.when(goes)
                def _():
                    @pl.when(comes)
                    def _():
                        arrive(buf, sem, (h, bz), kind)
                        buf[h, bz] = (total + wide(buf, h, bz)).astype(jnp.bfloat16)

                    @pl.when(jnp.logical_not(comes))
                    def _():
                        buf[h, bz] = total.astype(jnp.bfloat16)

                send(buf.at[h, bz], buf, sem, (h, bz), kind, goes)

    for turn in range(NZ + 2):
        if turn < NZ:
            pair(turn)
        if 0 <= turn - 1 < NZ:
            across(turn - 1)
        if 0 <= turn - 2 < NZ:
            along(turn - 2)
    for h in range(2):
        mine = x if h == 0 else y
        total = (
            wide(first_buf, h, z, mine)
            + wide(core_buf, h, chip_of(z, x, y))
            + wide(second_buf, h, z)
        )

        @pl.when(z == 0)
        def _():
            arrive(down_buf, down_sem, (h, z), Z_DOWN)
            out_ref[rows(h)] = (total + wide(down_buf, h, z)).astype(jnp.bfloat16)

        @pl.when(z == NZ - 1)
        def _():
            arrive(up_buf, up_sem, (h, z), Z_UP)
            out_ref[rows(h)] = (total + wide(up_buf, h, z)).astype(jnp.bfloat16)

        @pl.when(jnp.logical_and(z > 0, z < NZ - 1))
        def _():
            arrive(down_buf, down_sem, (h, z), Z_DOWN)
            arrive(up_buf, up_sem, (h, z), Z_UP)
            both = wide(up_buf, h, z) + wide(down_buf, h, z)
            out_ref[rows(h)] = (total + both).astype(jnp.bfloat16)

    for wait in sent:
        wait()


def reduce_plots(terms):
    length = terms.shape[1]
    half = length // 2

    def blocks(*lead):
        return pltpu.VMEM((*lead, half, D), jnp.bfloat16)

    return pl.pallas_call(
        reduce_kernel,
        out_shape=jax.ShapeDtypeStruct((length, D), jnp.bfloat16),
        in_specs=[pl.BlockSpec(memory_space=pltpu.VMEM)],
        out_specs=pl.BlockSpec(memory_space=pltpu.VMEM),
        scratch_shapes=[
            blocks(2, CHIPS),
            blocks(2, NZ, 2),
            blocks(2, NZ),
            blocks(2, NZ),
            blocks(2, NZ),
            pltpu.SemaphoreType.DMA((2, 2, CHIPS)),
            pltpu.SemaphoreType.DMA((2, 2, NZ, 2)),
            pltpu.SemaphoreType.DMA((2, 2, NZ)),
            pltpu.SemaphoreType.DMA((2, 2, NZ)),
            pltpu.SemaphoreType.DMA((2, 2, NZ)),
        ],
        compiler_params=pltpu.CompilerParams(
            collective_id=1, has_side_effects=True, vmem_limit_bytes=48 * 1024 * 1024
        ),
    )(terms)


def slot_positions(crop_ids, capacity):
    length = crop_ids.shape[0]
    same = crop_ids[:, None] == crop_ids[None, :]
    earlier = jnp.arange(length)[None, :] < jnp.arange(length)[:, None]
    slot_ids = jnp.sum(jnp.logical_and(same, earlier).astype(jnp.int32), axis=1)
    return crop_ids * capacity + slot_ids


def routed_experts(routed, length, w_gate, w_up, w_down):
    capacity = length // 4
    plots = CHIPS * NC
    local_count = w_gate.shape[0]
    tokens = gather_plots(routed)
    everywhere = tokens[:, length, :length].astype(jnp.int32)
    held = local_count * capacity
    slots = lax.axis_index("expert") * held + jnp.arange(held, dtype=jnp.int32)
    select = (everywhere[:, None, :] == slots[None, :, None]).astype(jnp.bfloat16)
    select = select.reshape(plots, local_count, capacity, length)
    packed = jnp.einsum(
        "pjct,ptd->jpcd", jnp.pad(select, ((0, 0),) * 3 + ((0, EXTRA),)), tokens, preferred_element_type=jnp.float32
    ).astype(jnp.bfloat16)
    packed = packed.reshape(local_count, plots * capacity, D)
    gate_act = jnp.einsum("jrd,jdf->jrf", packed, w_gate, preferred_element_type=jnp.float32)
    up_act = jnp.einsum("jrd,jdf->jrf", packed, w_up, preferred_element_type=jnp.float32)
    hidden = (jax.nn.silu(gate_act) * up_act).astype(jnp.bfloat16)
    term = jnp.einsum("jrf,jfd->jrd", hidden, w_down, preferred_element_type=jnp.float32)
    term = term.astype(jnp.bfloat16).reshape(local_count, plots, capacity, D)
    by_token = jnp.einsum(
        "pjct,jpcd->ptd", select, term, preferred_element_type=jnp.float32
    ).astype(jnp.bfloat16)
    return reduce_plots(by_token)


def rms_scale(values, width_eps):
    return lax.rsqrt(jnp.mean(values * values, axis=-1, keepdims=True) + width_eps)


def spread(buffers):
    return lax.all_gather(buffers, "dp", axis=0, tiled=True)


def deliver(buffers):
    return lax.all_to_all(buffers, "expert", split_axis=1, concat_axis=1, tiled=True)


def attend_kernel(
    tokens_ref,
    column_ref,
    line_ref,
    position_ref,
    attn_gain_ref,
    query_ref,
    key_ref,
    value_ref,
    head_gain_ref,
    w_out_ref,
    moe_gain_ref,
    resid_ref,
    routed_ref,
    normed_ref,
    total_ref,
):
    step = pl.program_id(0)
    length = tokens_ref.shape[0]

    @pl.when(step == 0)
    def _():
        widened = tokens_ref[...].astype(jnp.float32)
        scaled = widened * rms_scale(widened, 1e-05) * attn_gain_ref[...].astype(jnp.float32)
        normed_ref[...] = scaled.astype(jnp.bfloat16)
        total_ref[...] = widened

    def project(ref):
        return jnp.dot(
            normed_ref[...], ref[...], preferred_element_type=jnp.float32
        ).astype(jnp.bfloat16)

    query, key_vecs, value_vecs = project(query_ref), project(key_ref), project(value_ref)
    lanes = 2 * HEAD_DIM
    first = lax.broadcasted_iota(jnp.int32, (length, lanes), 1) < HEAD_DIM
    later = lax.broadcasted_iota(jnp.int32, (length, length), 0)
    causal = later >= lax.broadcasted_iota(jnp.int32, (length, length), 1)
    outcome = []
    for pair in range(query.shape[1] // lanes):
        cut = slice(pair * lanes, (pair + 1) * lanes)
        mixed = []
        for side in range(2):
            head = 2 * pair + side
            mask = first if side == 0 else jnp.logical_not(first)
            chosen = jnp.where(mask, query[:, cut], jnp.zeros((), jnp.bfloat16))
            scores = lax.dot_general(
                chosen,
                key_vecs[:, cut],
                (((1,), (1,)), ((), ())),
                preferred_element_type=jnp.float32,
            )
            gap = column_ref[0, :, head : head + 1] - line_ref[0, head : head + 1, :]
            weighted = scores * jnp.exp(jnp.where(causal, gap, -jnp.inf))
            coarse = weighted.astype(jnp.bfloat16)
            fine = (weighted - coarse.astype(jnp.float32)).astype(jnp.bfloat16)
            mixed.append(
                jnp.dot(coarse, value_vecs[:, cut], preferred_element_type=jnp.float32)
                + jnp.dot(fine, value_vecs[:, cut], preferred_element_type=jnp.float32)
            )
        both = jnp.where(first, mixed[0], mixed[1])
        square = both * both
        scale = [
            lax.rsqrt(
                jnp.sum(jnp.where(mask, square, 0.0), axis=-1, keepdims=True) / HEAD_DIM + 1e-05
            )
            for mask in (first, jnp.logical_not(first))
        ]
        gain = head_gain_ref[:, cut].astype(jnp.float32)
        outcome.append((both * jnp.where(first, scale[0], scale[1]) * gain).astype(jnp.bfloat16))
    total_ref[...] += jnp.dot(
        jnp.concatenate(outcome, axis=1), w_out_ref[...], preferred_element_type=jnp.float32
    )

    @pl.when(step == pl.num_programs(0) - 1)
    def _():
        resid = total_ref[...].astype(jnp.bfloat16)
        resid_ref[...] = resid
        wide = resid.astype(jnp.float32)
        scaled = wide * rms_scale(wide, 1e-05) * moe_gain_ref[...].astype(jnp.float32)
        routed_ref[:length, :] = scaled.astype(jnp.bfloat16)
        extra = routed_ref.shape[0] - length
        routed_ref[length:, :] = jnp.zeros((extra, D), jnp.bfloat16)
        routed_ref[length:, :length] = jnp.broadcast_to(
            position_ref[...].astype(jnp.float32), (extra, length)
        ).astype(jnp.bfloat16)


def attend(
    tokens, forget, position, attn_gain, w_query, w_key, w_value, head_gain, w_out, moe_gain
):
    length = tokens.shape[0]
    steps = 6
    width = D // steps
    cumulative = jnp.cumsum(forget, axis=0)
    line = cumulative.T.reshape(steps, HEADS // steps, length)
    column = jnp.transpose(line, (0, 2, 1))

    def whole(*shape):
        return pl.BlockSpec(shape, lambda j: (0,) * len(shape))

    columns = pl.BlockSpec((D, width), lambda j: (0, j))
    return pl.pallas_call(
        attend_kernel,
        grid=(steps,),
        out_shape=(
            jax.ShapeDtypeStruct((length, D), jnp.bfloat16),
            jax.ShapeDtypeStruct((length + EXTRA, D), jnp.bfloat16),
        ),
        in_specs=[
            whole(length, D),
            pl.BlockSpec((1, length, HEADS // steps), lambda j: (j, 0, 0)),
            pl.BlockSpec((1, HEADS // steps, length), lambda j: (j, 0, 0)),
            whole(1, length),
            whole(1, D),
            columns,
            columns,
            columns,
            pl.BlockSpec((1, width), lambda j: (0, j)),
            pl.BlockSpec((width, D), lambda j: (j, 0)),
            whole(1, D),
        ],
        out_specs=(whole(length, D), whole(length + EXTRA, D)),
        scratch_shapes=[
            pltpu.VMEM((length, D), jnp.bfloat16),
            pltpu.VMEM((length, D), jnp.float32),
        ],
        compiler_params=pltpu.CompilerParams(vmem_limit_bytes=32 * 1024 * 1024),
    )(
        tokens,
        column,
        line,
        position.reshape(1, length),
        attn_gain.reshape(1, D),
        w_query,
        w_key,
        w_value,
        head_gain.reshape(1, D),
        w_out,
        moe_gain.reshape(1, D),
    )


def on_device(
    x_spans,
    crops,
    decay,
    attn_gain,
    w_query,
    w_key,
    w_value,
    head_gain,
    w_out,
    moe_gain,
    w_gate,
    w_up,
    w_down,
):
    arrived = lax.all_to_all(x_spans, "dp", split_axis=1, concat_axis=0, tiled=True)
    length = arrived.shape[0] * arrived.shape[3]
    tokens = arrived.reshape(length, D)
    forget = decay.reshape(length, HEADS)
    crop_ids = crops.reshape(length)
    capacity = length // 4
    position = slot_positions(crop_ids, capacity)
    resid, routed = attend(
        tokens, forget, position, attn_gain, w_query, w_key, w_value, head_gain, w_out, moe_gain
    )
    resid_wide = resid.astype(jnp.float32)
    if lax.axis_size("dp") == NZ * NX and lax.axis_size("expert") == NY * NC:
        expert_out = routed_experts(routed, length, w_gate, w_up, w_down)
        layer_sum = (resid_wide + expert_out.astype(jnp.float32)).astype(jnp.bfloat16)
        return layer_sum.reshape(1, 1, length, D)
    select = (jnp.arange(EXPERTS * capacity, dtype=jnp.int32)[:, None] == position[None, :]).astype(
        jnp.bfloat16
    )
    packed = jnp.dot(select, routed[:length], preferred_element_type=jnp.float32).astype(jnp.bfloat16)
    owners = lax.axis_size("expert")
    local_count = w_gate.shape[0]
    outgoing = packed.reshape(1, owners, EXPERTS * capacity // owners, D)
    gathered = spread(deliver(outgoing))
    sources = gathered.shape[0]
    grouped = gathered.reshape(sources, owners, local_count, capacity, D)
    gate_act = jnp.einsum("sojcd,jdf->sojcf", grouped, w_gate, preferred_element_type=jnp.float32)
    up_act = jnp.einsum("sojcd,jdf->sojcf", grouped, w_up, preferred_element_type=jnp.float32)
    hidden = (jax.nn.silu(gate_act) * up_act).astype(jnp.bfloat16)
    term = jnp.einsum("sojcf,jfd->sojcd", hidden, w_down, preferred_element_type=jnp.float32)
    summed = lax.psum_scatter(
        term.reshape(1 * lax.axis_size("dp"), owners, local_count * capacity, D).astype(
            jnp.bfloat16
        ),
        "dp",
        scatter_dimension=0,
        tiled=True,
    )
    own_sums = summed[0]
    returned = lax.all_to_all(own_sums, "expert", split_axis=0, concat_axis=0, tiled=True)
    flat_back = returned.reshape(EXPERTS * capacity, D)
    expert_out = jnp.einsum("pl,pd->ld", select, flat_back, preferred_element_type=jnp.float32)
    layer_sum = (resid_wide + expert_out).astype(jnp.bfloat16)
    return layer_sum.reshape(1, 1, length, D)


def solution(mesh):
    return jax.shard_map(
        on_device,
        mesh=mesh,
        in_specs=(
            P("dp", None, "expert", None, None),
            P("dp", "expert", None, None),
            P("dp", "expert", None, None),
            P(),
            P(),
            P(),
            P(),
            P(),
            P(),
            P(),
            P("expert", None, "dp"),
            P("expert", None, "dp"),
            P("expert", "dp", None),
        ),
        out_specs=P("dp", "expert", None, None),
        check_vma=False,
    )
```

```python
import jax
import jax.numpy as jnp
from jax import lax
from jax.experimental import pallas as pl
from jax.experimental.pallas import tpu as pltpu
from jax.sharding import PartitionSpec as P

D = 1536
HEADS = 24
HEAD_DIM = 64
EXPERTS = 8
EXTRA = 16
NZ = 4
NX = 2
NY = 2
NC = 2
CHIPS = NZ * NX * NY
Z_UP, Z_DOWN, BY_X, BY_Y, CORE = range(5)


def place():
    dp, expert = lax.axis_index("dp"), lax.axis_index("expert")
    return dp // NX, dp % NX, expert // NC, expert % NC


def device(z, x, y, c):
    return (z * NX + x, y * NC + c)


def plot_of(z, x, y, c):
    return (z * NX + x) * (NY * NC) + y * NC + c


def chip_of(z, x, y):
    return (z * NX + x) * NY + y


def partner(kind, z, x, y, c):
    if kind == Z_UP:
        return device(z + 1, x, y, c)
    if kind == Z_DOWN:
        return device(z - 1, x, y, c)
    if kind == BY_X:
        return device(z, 1 - x, y, c)
    if kind == BY_Y:
        return device(z, x, 1 - y, c)
    return device(z, x, y, 1 - c)


def only_if(condition, body):
    if condition is None:
        body()
    else:
        pl.when(condition)(body)


def exists(kind, z):
    return {Z_UP: z < NZ - 1, Z_DOWN: z > 0}.get(kind)


def greet(z, x, y, c):
    barrier = pltpu.get_barrier_semaphore()
    for kind in range(5):

        def signal(kind=kind):
            pl.semaphore_signal(
                barrier,
                inc=1,
                device_id=partner(kind, z, x, y, c),
                device_id_type=pl.DeviceIdType.MESH,
            )

        only_if(exists(kind, z), signal)
    pl.semaphore_wait(barrier, 3 + jnp.where(z > 0, 1, 0) + jnp.where(z < NZ - 1, 1, 0))


def gather_kernel(own_ref, out_ref, send_sem, recv_sem, core_sem, local_sem):
    z, x, y, c = place()
    length = own_ref.shape[0]
    half = length // (2 * EXTRA) * EXTRA
    greet(z, x, y, c)
    sent = []

    def rows(h):
        return pl.ds(h * half, half if h == 0 else length - half)

    def copy(h, kind, bz, bx, by, own):
        chip = chip_of(bz, bx, by)
        target = out_ref.at[plot_of(bz, bx, by, c), rows(h)]
        return pltpu.make_async_remote_copy(
            src_ref=own_ref.at[rows(h)] if own else target,
            dst_ref=target,
            send_sem=send_sem.at[h, kind, chip],
            recv_sem=(core_sem if kind == CORE else recv_sem).at[h, chip],
            device_id=partner(kind, z, x, y, c),
            device_id_type=pl.DeviceIdType.MESH,
        )

    def send(h, kind, bz, bx, by, guard, own=False):
        def both(action):
            def body():
                def inner():
                    action(copy(h, kind, bz, bx, by, own))

                only_if(exists(kind, z), inner)

            only_if(guard, body)

        both(lambda made: made.start())
        sent.append(lambda: both(lambda made: made.wait_send()))

    def arrive(h, bz, bx, by, guard):
        only_if(guard, lambda: copy(h, BY_X, bz, bx, by, False).wait_recv())

    stay = pltpu.make_async_copy(own_ref, out_ref.at[plot_of(z, x, y, c)], local_sem)
    stay.start()
    middle = (BY_X, BY_Y)
    last = (BY_Y, BY_X)
    for h in range(2):
        for kind in (Z_UP, Z_DOWN, middle[h], last[h], CORE):
            send(h, kind, z, x, y, None, own=True)

    def spots(step):
        if step == 0:
            return [(z, None, None)]
        return [(z - step, z - step >= 0, Z_UP), (z + step, z + step < NZ, Z_DOWN)]

    for turn in range(NZ + 2):
        if 1 <= turn < NZ:
            for bz, guard, way in spots(turn):
                for h in range(2):
                    arrive(h, bz, x, y, guard)
                    for kind in (way, middle[h], last[h], CORE):
                        send(h, kind, bz, x, y, guard)
        if 0 <= turn - 1 < NZ:
            for bz, guard, _ in spots(turn - 1):
                for h in range(2):
                    bx, by = (1 - x, y) if h == 0 else (x, 1 - y)
                    arrive(h, bz, bx, by, guard)
                    for kind in (last[h], CORE):
                        send(h, kind, bz, bx, by, guard)
        if 0 <= turn - 2 < NZ:
            for bz, guard, _ in spots(turn - 2):
                for h in range(2):
                    for bx, by in ((x, 1 - y), (1 - x, 1 - y)) if h == 0 else ((1 - x, y), (1 - x, 1 - y)):
                        arrive(h, bz, bx, by, guard)
                        send(h, CORE, bz, bx, by, guard)
    for chip in range(CHIPS):
        bz, bx, by = chip // (NX * NY), chip // NY % NX, chip % NY
        for h in range(2):
            landed = out_ref.at[plot_of(bz, bx, by, 1 - c), rows(h)]
            pltpu.make_async_remote_copy(
                src_ref=landed,
                dst_ref=landed,
                send_sem=send_sem.at[h, CORE, chip],
                recv_sem=core_sem.at[h, chip],
                device_id=partner(CORE, z, x, y, c),
                device_id_type=pl.DeviceIdType.MESH,
            ).wait_recv()
    for wait in sent:
        wait()
    stay.wait()


def gather_plots(own):
    length = own.shape[0]
    plots = CHIPS * NC
    return pl.pallas_call(
        gather_kernel,
        out_shape=jax.ShapeDtypeStruct((plots, length, D), jnp.bfloat16),
        in_specs=[pl.BlockSpec(memory_space=pltpu.VMEM)],
        out_specs=pl.BlockSpec(memory_space=pl.ANY),
        scratch_shapes=[
            pltpu.SemaphoreType.DMA((2, 5, CHIPS)),
            pltpu.SemaphoreType.DMA((2, CHIPS)),
            pltpu.SemaphoreType.DMA((2, CHIPS)),
            pltpu.SemaphoreType.DMA,
        ],
        compiler_params=pltpu.CompilerParams(collective_id=0, has_side_effects=True),
    )(own)


def reduce_kernel(
    terms_ref,
    out_ref,
    core_buf,
    first_buf,
    second_buf,
    up_buf,
    down_buf,
    core_sem,
    first_sem,
    second_sem,
    up_sem,
    down_sem,
):
    z, x, y, c = place()
    half = out_ref.shape[0] // 2
    greet(z, x, y, c)
    sent = []

    def rows(h):
        return pl.ds(h * half, half)

    def move(src, buf, sem, index, kind):
        return pltpu.make_async_remote_copy(
            src_ref=src,
            dst_ref=buf.at[index],
            send_sem=sem.at[(0, *index)],
            recv_sem=sem.at[(1, *index)],
            device_id=partner(kind, z, x, y, c),
            device_id_type=pl.DeviceIdType.MESH,
        )

    def send(src, buf, sem, index, kind, guard=None):
        only_if(guard, lambda: move(src, buf, sem, index, kind).start())
        sent.append(lambda: only_if(guard, lambda: move(src, buf, sem, index, kind).wait_send()))

    def arrive(buf, sem, index, kind):
        move(buf.at[index], buf, sem, index, kind).wait_recv()

    def wide(ref, *index):
        return ref[index].astype(jnp.float32)

    low = jnp.where(z < NZ // 2, 1, 0)

    def layer(turn):
        return low * (NZ - 1 - turn) + (1 - low) * turn

    def spot(h, first_other, second_other):
        first, second = (y, x) if h == 0 else (x, y)
        first = 1 - first if first_other else first
        second = 1 - second if second_other else second
        return (second, first) if h == 0 else (first, second)

    order = ((1, 1), (1, 0), (0, 1), (0, 0))
    first_kind, second_kind = (BY_Y, BY_X), (BY_X, BY_Y)
    for turn in range(NZ):
        for first_other, second_other in order:
            for h in range(2):
                bx, by = spot(h, first_other, second_other)
                bz = layer(turn)
                send(
                    terms_ref.at[plot_of(bz, bx, by, 1 - c), rows(h)],
                    core_buf,
                    core_sem,
                    (h, chip_of(bz, bx, by)),
                    CORE,
                )

    def pair(turn):
        bz = layer(turn)
        for first_other, second_other in order:
            for h in range(2):
                bx, by = spot(h, first_other, second_other)
                index = (h, chip_of(bz, bx, by))
                arrive(core_buf, core_sem, index, CORE)
                total = wide(core_buf, *index) + wide(
                    terms_ref, plot_of(bz, bx, by, c), rows(h)
                )
                core_buf[index] = total.astype(jnp.bfloat16)
                if first_other:
                    second = bx if h == 0 else by
                    send(
                        core_buf.at[index], first_buf, first_sem, (h, bz, second), first_kind[h]
                    )

    def across(turn):
        bz = layer(turn)
        for h in range(2):
            bx, by = spot(h, 0, 1)
            index = (h, bz, bx if h == 0 else by)
            arrive(first_buf, first_sem, index, first_kind[h])
            total = wide(first_buf, *index) + wide(core_buf, h, chip_of(bz, bx, by))
            first_buf[index] = total.astype(jnp.bfloat16)
            send(first_buf.at[index], second_buf, second_sem, (h, bz), second_kind[h])

    def along(turn):
        bz = layer(turn)
        for h in range(2):
            bx, by = spot(h, 0, 0)
            index = (h, bz, bx if h == 0 else by)
            arrive(first_buf, first_sem, index, first_kind[h])
            arrive(second_buf, second_sem, (h, bz), second_kind[h])
            total = (
                wide(first_buf, *index)
                + wide(core_buf, h, chip_of(bz, bx, by))
                + wide(second_buf, h, bz)
            )
            for buf, sem, kind, goes, comes in (
                (up_buf, up_sem, Z_UP, bz > z, z > 0),
                (down_buf, down_sem, Z_DOWN, bz < z, z < NZ - 1),
            ):

                @pl.when(goes)
                def _():
                    @pl.when(comes)
                    def _():
                        arrive(buf, sem, (h, bz), kind)
                        buf[h, bz] = (total + wide(buf, h, bz)).astype(jnp.bfloat16)

                    @pl.when(jnp.logical_not(comes))
                    def _():
                        buf[h, bz] = total.astype(jnp.bfloat16)

                send(buf.at[h, bz], buf, sem, (h, bz), kind, goes)

    for turn in range(NZ + 2):
        if turn < NZ:
            pair(turn)
        if 0 <= turn - 1 < NZ:
            across(turn - 1)
        if 0 <= turn - 2 < NZ:
            along(turn - 2)
    for h in range(2):
        mine = x if h == 0 else y
        total = (
            wide(first_buf, h, z, mine)
            + wide(core_buf, h, chip_of(z, x, y))
            + wide(second_buf, h, z)
        )

        @pl.when(z == 0)
        def _():
            arrive(down_buf, down_sem, (h, z), Z_DOWN)
            out_ref[rows(h)] = (total + wide(down_buf, h, z)).astype(jnp.bfloat16)

        @pl.when(z == NZ - 1)
        def _():
            arrive(up_buf, up_sem, (h, z), Z_UP)
            out_ref[rows(h)] = (total + wide(up_buf, h, z)).astype(jnp.bfloat16)

        @pl.when(jnp.logical_and(z > 0, z < NZ - 1))
        def _():
            arrive(down_buf, down_sem, (h, z), Z_DOWN)
            arrive(up_buf, up_sem, (h, z), Z_UP)
            both = wide(up_buf, h, z) + wide(down_buf, h, z)
            out_ref[rows(h)] = (total + both).astype(jnp.bfloat16)

    for wait in sent:
        wait()


def reduce_plots(terms):
    length = terms.shape[1]
    half = length // 2

    def blocks(*lead):
        return pltpu.VMEM((*lead, half, D), jnp.bfloat16)

    return pl.pallas_call(
        reduce_kernel,
        out_shape=jax.ShapeDtypeStruct((length, D), jnp.bfloat16),
        in_specs=[pl.BlockSpec(memory_space=pltpu.VMEM)],
        out_specs=pl.BlockSpec(memory_space=pltpu.VMEM),
        scratch_shapes=[
            blocks(2, CHIPS),
            blocks(2, NZ, 2),
            blocks(2, NZ),
            blocks(2, NZ),
            blocks(2, NZ),
            pltpu.SemaphoreType.DMA((2, 2, CHIPS)),
            pltpu.SemaphoreType.DMA((2, 2, NZ, 2)),
            pltpu.SemaphoreType.DMA((2, 2, NZ)),
            pltpu.SemaphoreType.DMA((2, 2, NZ)),
            pltpu.SemaphoreType.DMA((2, 2, NZ)),
        ],
        compiler_params=pltpu.CompilerParams(
            collective_id=1, has_side_effects=True, vmem_limit_bytes=48 * 1024 * 1024
        ),
    )(terms)


def slot_positions(crop_ids, capacity):
    length = crop_ids.shape[0]
    same = crop_ids[:, None] == crop_ids[None, :]
    earlier = jnp.arange(length)[None, :] < jnp.arange(length)[:, None]
    slot_ids = jnp.sum(jnp.logical_and(same, earlier).astype(jnp.int32), axis=1)
    return crop_ids * capacity + slot_ids


def experts_kernel(
    base_ref, tokens_ref, w_gate_ref, w_up_ref, w_down_ref, out_ref, packed_ref, term_ref
):
    plots, length = out_ref.shape[0], out_ref.shape[1]
    experts = w_gate_ref.shape[0]
    capacity = packed_ref.shape[1] // plots
    held = experts * capacity
    slots = lax.broadcasted_iota(jnp.int32, (held, length), 0) + base_ref[0]

    def select(plot):
        position = tokens_ref[plot, length:, :length].astype(jnp.float32)[:1]
        hit = slots == position.astype(jnp.int32)
        return jnp.where(hit, 1.0, 0.0).astype(jnp.bfloat16)

    for plot in range(plots):
        rows = jnp.dot(
            select(plot), tokens_ref[plot, :length, :], preferred_element_type=jnp.float32
        ).astype(jnp.bfloat16)
        for j in range(experts):
            packed_ref[j, plot * capacity : (plot + 1) * capacity, :] = rows[
                j * capacity : (j + 1) * capacity
            ]
    for j in range(experts):
        packed = packed_ref[j]
        gate_act = jnp.dot(packed, w_gate_ref[j], preferred_element_type=jnp.float32)
        up_act = jnp.dot(packed, w_up_ref[j], preferred_element_type=jnp.float32)
        hidden = (gate_act / (1.0 + jnp.exp(-gate_act)) * up_act).astype(jnp.bfloat16)
        term_ref[j] = jnp.dot(
            hidden, w_down_ref[j], preferred_element_type=jnp.float32
        ).astype(jnp.bfloat16)
    for plot in range(plots):
        cut = slice(plot * capacity, (plot + 1) * capacity)
        term = jnp.concatenate([term_ref[j, cut, :] for j in range(experts)], axis=0)
        out_ref[plot] = lax.dot_general(
            select(plot), term, (((0,), (0,)), ((), ())), preferred_element_type=jnp.float32
        ).astype(jnp.bfloat16)


def routed_experts(routed, length, w_gate, w_up, w_down):
    capacity = length // 4
    plots = CHIPS * NC
    group = plots // NZ
    local_count, _, width = w_gate.shape
    tokens = gather_plots(routed)
    base = (lax.axis_index("expert") * (local_count * capacity)).astype(jnp.int32).reshape(1)

    def resident(*shape):
        return pl.BlockSpec(shape, lambda i: (0, 0, 0), pipeline_mode=pl.Buffered(1))

    by_token = pl.pallas_call(
        experts_kernel,
        grid=(NZ,),
        out_shape=jax.ShapeDtypeStruct((plots, length, D), jnp.bfloat16),
        in_specs=[
            pl.BlockSpec(memory_space=pltpu.SMEM),
            pl.BlockSpec((group, length + EXTRA, D), lambda i: (i, 0, 0)),
            resident(local_count, D, width),
            resident(local_count, D, width),
            resident(local_count, width, D),
        ],
        out_specs=pl.BlockSpec((group, length, D), lambda i: (i, 0, 0)),
        scratch_shapes=[
            pltpu.VMEM((local_count, group * capacity, D), jnp.bfloat16),
            pltpu.VMEM((local_count, group * capacity, D), jnp.bfloat16),
        ],
        compiler_params=pltpu.CompilerParams(vmem_limit_bytes=56 * 1024 * 1024),
    )(base, tokens, w_gate, w_up, w_down)
    return reduce_plots(by_token)


def rms_scale(values, width_eps):
    return lax.rsqrt(jnp.mean(values * values, axis=-1, keepdims=True) + width_eps)


def spread(buffers):
    return lax.all_gather(buffers, "dp", axis=0, tiled=True)


def deliver(buffers):
    return lax.all_to_all(buffers, "expert", split_axis=1, concat_axis=1, tiled=True)


def attend_kernel(
    tokens_ref,
    column_ref,
    line_ref,
    position_ref,
    attn_gain_ref,
    query_ref,
    key_ref,
    value_ref,
    head_gain_ref,
    w_out_ref,
    moe_gain_ref,
    resid_ref,
    routed_ref,
    normed_ref,
    total_ref,
):
    step = pl.program_id(0)
    length = tokens_ref.shape[0]

    @pl.when(step == 0)
    def _():
        widened = tokens_ref[...].astype(jnp.float32)
        scaled = widened * rms_scale(widened, 1e-05) * attn_gain_ref[...].astype(jnp.float32)
        normed_ref[...] = scaled.astype(jnp.bfloat16)
        total_ref[...] = widened

    def project(ref):
        return jnp.dot(
            normed_ref[...], ref[...], preferred_element_type=jnp.float32
        ).astype(jnp.bfloat16)

    query, key_vecs, value_vecs = project(query_ref), project(key_ref), project(value_ref)
    lanes = 2 * HEAD_DIM
    first = lax.broadcasted_iota(jnp.int32, (length, lanes), 1) < HEAD_DIM
    later = lax.broadcasted_iota(jnp.int32, (length, length), 0)
    causal = later >= lax.broadcasted_iota(jnp.int32, (length, length), 1)
    outcome = []
    for pair in range(query.shape[1] // lanes):
        cut = slice(pair * lanes, (pair + 1) * lanes)
        mixed = []
        for side in range(2):
            head = 2 * pair + side
            mask = first if side == 0 else jnp.logical_not(first)
            chosen = jnp.where(mask, query[:, cut], jnp.zeros((), jnp.bfloat16))
            scores = lax.dot_general(
                chosen,
                key_vecs[:, cut],
                (((1,), (1,)), ((), ())),
                preferred_element_type=jnp.float32,
            )
            gap = column_ref[0, :, head : head + 1] - line_ref[0, head : head + 1, :]
            weighted = scores * jnp.exp(jnp.where(causal, gap, -jnp.inf))
            coarse = weighted.astype(jnp.bfloat16)
            fine = (weighted - coarse.astype(jnp.float32)).astype(jnp.bfloat16)
            mixed.append(
                jnp.dot(coarse, value_vecs[:, cut], preferred_element_type=jnp.float32)
                + jnp.dot(fine, value_vecs[:, cut], preferred_element_type=jnp.float32)
            )
        both = jnp.where(first, mixed[0], mixed[1])
        square = both * both
        scale = [
            lax.rsqrt(
                jnp.sum(jnp.where(mask, square, 0.0), axis=-1, keepdims=True) / HEAD_DIM + 1e-05
            )
            for mask in (first, jnp.logical_not(first))
        ]
        gain = head_gain_ref[:, cut].astype(jnp.float32)
        outcome.append((both * jnp.where(first, scale[0], scale[1]) * gain).astype(jnp.bfloat16))
    total_ref[...] += jnp.dot(
        jnp.concatenate(outcome, axis=1), w_out_ref[...], preferred_element_type=jnp.float32
    )

    @pl.when(step == pl.num_programs(0) - 1)
    def _():
        resid = total_ref[...].astype(jnp.bfloat16)
        resid_ref[...] = resid
        wide = resid.astype(jnp.float32)
        scaled = wide * rms_scale(wide, 1e-05) * moe_gain_ref[...].astype(jnp.float32)
        routed_ref[:length, :] = scaled.astype(jnp.bfloat16)
        extra = routed_ref.shape[0] - length
        routed_ref[length:, :] = jnp.zeros((extra, D), jnp.bfloat16)
        routed_ref[length:, :length] = jnp.broadcast_to(
            position_ref[...].astype(jnp.float32), (extra, length)
        ).astype(jnp.bfloat16)


def attend(
    tokens, forget, position, attn_gain, w_query, w_key, w_value, head_gain, w_out, moe_gain
):
    length = tokens.shape[0]
    steps = 6
    width = D // steps
    cumulative = jnp.cumsum(forget, axis=0)
    line = cumulative.T.reshape(steps, HEADS // steps, length)
    column = jnp.transpose(line, (0, 2, 1))

    def whole(*shape):
        return pl.BlockSpec(shape, lambda j: (0,) * len(shape))

    columns = pl.BlockSpec((D, width), lambda j: (0, j))
    return pl.pallas_call(
        attend_kernel,
        grid=(steps,),
        out_shape=(
            jax.ShapeDtypeStruct((length, D), jnp.bfloat16),
            jax.ShapeDtypeStruct((length + EXTRA, D), jnp.bfloat16),
        ),
        in_specs=[
            whole(length, D),
            pl.BlockSpec((1, length, HEADS // steps), lambda j: (j, 0, 0)),
            pl.BlockSpec((1, HEADS // steps, length), lambda j: (j, 0, 0)),
            whole(1, length),
            whole(1, D),
            columns,
            columns,
            columns,
            pl.BlockSpec((1, width), lambda j: (0, j)),
            pl.BlockSpec((width, D), lambda j: (j, 0)),
            whole(1, D),
        ],
        out_specs=(whole(length, D), whole(length + EXTRA, D)),
        scratch_shapes=[
            pltpu.VMEM((length, D), jnp.bfloat16),
            pltpu.VMEM((length, D), jnp.float32),
        ],
        compiler_params=pltpu.CompilerParams(vmem_limit_bytes=56 * 1024 * 1024),
    )(
        tokens,
        column,
        line,
        position.reshape(1, length),
        attn_gain.reshape(1, D),
        w_query,
        w_key,
        w_value,
        head_gain.reshape(1, D),
        w_out,
        moe_gain.reshape(1, D),
    )


def on_device(
    x_spans,
    crops,
    decay,
    attn_gain,
    w_query,
    w_key,
    w_value,
    head_gain,
    w_out,
    moe_gain,
    w_gate,
    w_up,
    w_down,
):
    arrived = lax.all_to_all(x_spans, "dp", split_axis=1, concat_axis=0, tiled=True)
    length = arrived.shape[0] * arrived.shape[3]
    tokens = arrived.reshape(length, D)
    forget = decay.reshape(length, HEADS)
    crop_ids = crops.reshape(length)
    capacity = length // 4
    position = slot_positions(crop_ids, capacity)
    resid, routed = attend(
        tokens, forget, position, attn_gain, w_query, w_key, w_value, head_gain, w_out, moe_gain
    )
    resid_wide = resid.astype(jnp.float32)
    if lax.axis_size("dp") == NZ * NX and lax.axis_size("expert") == NY * NC:
        expert_out = routed_experts(routed, length, w_gate, w_up, w_down)
        layer_sum = (resid_wide + expert_out.astype(jnp.float32)).astype(jnp.bfloat16)
        return layer_sum.reshape(1, 1, length, D)
    select = (jnp.arange(EXPERTS * capacity, dtype=jnp.int32)[:, None] == position[None, :]).astype(
        jnp.bfloat16
    )
    packed = jnp.dot(select, routed[:length], preferred_element_type=jnp.float32).astype(jnp.bfloat16)
    owners = lax.axis_size("expert")
    local_count = w_gate.shape[0]
    outgoing = packed.reshape(1, owners, EXPERTS * capacity // owners, D)
    gathered = spread(deliver(outgoing))
    sources = gathered.shape[0]
    grouped = gathered.reshape(sources, owners, local_count, capacity, D)
    gate_act = jnp.einsum("sojcd,jdf->sojcf", grouped, w_gate, preferred_element_type=jnp.float32)
    up_act = jnp.einsum("sojcd,jdf->sojcf", grouped, w_up, preferred_element_type=jnp.float32)
    hidden = (jax.nn.silu(gate_act) * up_act).astype(jnp.bfloat16)
    term = jnp.einsum("sojcf,jfd->sojcd", hidden, w_down, preferred_element_type=jnp.float32)
    summed = lax.psum_scatter(
        term.reshape(1 * lax.axis_size("dp"), owners, local_count * capacity, D).astype(
            jnp.bfloat16
        ),
        "dp",
        scatter_dimension=0,
        tiled=True,
    )
    own_sums = summed[0]
    returned = lax.all_to_all(own_sums, "expert", split_axis=0, concat_axis=0, tiled=True)
    flat_back = returned.reshape(EXPERTS * capacity, D)
    expert_out = jnp.einsum("pl,pd->ld", select, flat_back, preferred_element_type=jnp.float32)
    layer_sum = (resid_wide + expert_out).astype(jnp.bfloat16)
    return layer_sum.reshape(1, 1, length, D)


def solution(mesh):
    return jax.shard_map(
        on_device,
        mesh=mesh,
        in_specs=(
            P("dp", None, "expert", None, None),
            P("dp", "expert", None, None),
            P("dp", "expert", None, None),
            P(),
            P(),
            P(),
            P(),
            P(),
            P(),
            P(),
            P("expert", None, "dp"),
            P("expert", None, "dp"),
            P("expert", "dp", None),
        ),
        out_specs=P("dp", "expert", None, None),
        check_vma=False,
    )
```
